128 devices in a mesh: gx: 8 (over y, core), gy: 16 (over z, x).
Axes of the slice: x: 4, y: 4, z: 4, core: 2. Of those that a mesh axis runs over, the one named last changes fastest.
Arguments:
- model_state: float32 [200, 256, 2048], P(None, 'gx', 'gy'), may hold values from -6 to 6
- obs_cell: int32 [128, 2048], P(('gx', 'gy')), may hold values from 0 to 4095
- obs_count: int32 [128, 128], P(('gx', 'gy')), may hold values from 0 to 16, as said below
- obs_value: float32 [16, 262144], P(None, ('gx', 'gy')), may hold values from -6 to 6
- obs_weight: float32 [16, 262144], P(None, ('gx', 'gy')), may hold values from 0.25 to 4
- predictor: float32 [8, 262144], P(None, ('gx', 'gy')), may hold values from -6 to 6
- bias_coef: float32 [16, 8], replicated, may hold values from -3 to 3
- weight_in: float32 [768, 200], replicated, may hold values from -0.4375 to 0.4375
- bias_in: float32 [768], replicated, may hold values from -3 to 3
- weight_mid: float32 [768, 768], replicated, may hold values from -0.21875 to 0.21875
- bias_mid: float32 [768], replicated, may hold values from -3 to 3
- weight_out: float32 [16, 768], replicated, may hold values from -0.21875 to 0.21875
- bias_out: float32 [16], replicated, may hold values from -4 to 4
Outputs:
- gradient: float32 [200, 256, 2048], P(None, 'gx', 'gy')
- evolved: float32 [16, 262144], P(None, ('gx', 'gy'))
- bias_gradient: float32 [16, 8], replicated
The draws below stay inside these ranges and needn't reach their ends.
Inputs may be any that keep to these rules, and one draw needn't show every extreme that they name: obs_count[o, s] is how many of the 16 slots that owner o keeps for grid block s are used, from the first on; for some block s every owner uses all 16. `obs_cell`: a cell within a block is numbered row within the block times 128 plus column within the block.
All inputs are finite; a program needn't handle non-finite values.
Results may differ from the reference program's by a relative error of at most 0.000096.
Values sent between devices are 32-bit elements; how exact they have to be, the bound alone decides.
No kernel may reach another device: no remote copies, remote signals or barrier semaphores. Data moves between devices by JAX's collectives and lax.ppermute only.
A program may use at most 64 MiB of HBM per device.

```python
import math
import jax
import jax.numpy as jnp
from jax import lax

FEAT = 200
HID = 768
CH = 16
NPRED = 8
CX = 32
CY = 128
OBS_DEV = 2048
CAP = 16
NX = 256
NY = 2048
OBS_TOTAL = 262144
N_GY = 16
DEVICES = 128


def draw_obs_count(key, part):
    count_key, block_key = jax.random.split(jax.random.fold_in(key, 17))
    counts = jax.random.randint(count_key, (DEVICES, DEVICES), 0, CAP + 1)
    busy_block = jax.random.randint(block_key, (), 0, DEVICES)
    full_column = jnp.arange(DEVICES)[None, :] == busy_block
    return jnp.where(full_column, CAP, counts).astype(jnp.int32)


def touch_ends(entries, stream_key, least, high):
    longest = entries.shape.index(max(entries.shape))
    spots = []
    for shift in (0, 1):
        where = [jax.random.randint(jax.random.fold_in(stream_key, axis), (), 0, length) for axis, length in enumerate(entries.shape)]
        where[longest] = (where[longest] + shift) % entries.shape[longest]
        spots.append(tuple(where))
    return entries.at[spots[0]].set(least).at[spots[1]].set(high)


def block_levels(own_key, shape, pieces, smallest, largest):
    def one(dim, parts):
        draws = jax.random.uniform(jax.random.fold_in(jax.random.fold_in(own_key, 6), dim), (parts,), jnp.float32, smallest / len(pieces), largest / len(pieces))
        return jnp.repeat(jnp.exp(draws), shape[dim] // parts).reshape((-1,) + (1,) * (len(shape) - dim - 1))

    gain = one(*pieces[0])
    for cut in pieces[1:]:
        gain = gain * one(*cut)
    return gain


def noise(rng, extent, width, most, shards=(), kind=jnp.bfloat16):
    values = width * jax.random.normal(rng, extent, jnp.float32)
    if shards:
        values = values * block_levels(rng, extent, shards, -0.22, 0.18)
    return jnp.clip(values, -most, most).astype(kind)


def setup_inputs(seed: int = 0) -> dict:
    streams_of = jax.random.split(jax.random.key(seed), 14)
    return {
        "model_state": noise(streams_of[0], (FEAT, NX, NY), 1.0, 6.0, ((1, 8), (2, 16)), jnp.float32),
        "obs_cell": touch_ends(jax.random.randint(streams_of[1], (DEVICES, OBS_DEV), 0, CX * CY), jax.random.fold_in(streams_of[1], 1), 0, (CX * CY) - 1).astype(jnp.int32),
        "obs_count": draw_obs_count(jax.random.fold_in(streams_of[13], 71), 0),
        "obs_value": noise(streams_of[3], (CH, OBS_TOTAL), 1.0, 6.0, ((1, 128),), jnp.float32),
        "obs_weight": jnp.clip(jnp.exp(math.log(4.0) - 2.7725887 * jax.random.uniform(streams_of[4], (CH, OBS_TOTAL), jnp.float32) ** block_levels(streams_of[4], (CH, OBS_TOTAL), ((1, 128),), -0.2, 0.2)), 0.25, 4.0),
        "predictor": noise(streams_of[5], (NPRED, OBS_TOTAL), 1.0, 6.0, ((1, 128),), jnp.float32),
        "bias_coef": noise(streams_of[6], (CH, NPRED), 0.5, 3.0, (), jnp.float32),
        "weight_in": noise(streams_of[7], (HID, FEAT), FEAT ** -0.5, 0.4375, (), jnp.float32),
        "bias_in": noise(streams_of[8], (HID,), 0.5, 3.0, (), jnp.float32),
        "weight_mid": noise(streams_of[9], (HID, HID), HID ** -0.5, 0.21875, (), jnp.float32),
        "bias_mid": noise(streams_of[10], (HID,), 0.5, 3.0, (), jnp.float32),
        "weight_out": noise(streams_of[11], (CH, HID), HID ** -0.5, 0.21875, (), jnp.float32),
        "bias_out": noise(streams_of[12], (CH,), 1.0, 4.0, (), jnp.float32),
    }


def product(lhs_array, rhs_array):
    return jnp.dot(lhs_array, rhs_array, preferred_element_type=jnp.float32, precision=lax.Precision.HIGHEST)


def observe(profile, obs_rows, weight_rows, pred_rows, bias_coef, weight_in, bias_in, weight_mid, bias_mid, weight_out, bias_out):
    hidden_in = jnp.tanh(product(weight_in, profile) + bias_in[:, None])
    hidden_mid = jnp.tanh(product(weight_mid, hidden_in) + bias_mid[:, None])
    model_out = product(weight_out, hidden_mid) + bias_out[:, None] + product(bias_coef, pred_rows)
    residual_term = weight_rows * (model_out - obs_rows)
    back_mid = product(weight_out.T, residual_term) * (1.0 - hidden_mid * hidden_mid)
    back_in = product(weight_mid.T, back_mid) * (1.0 - hidden_in * hidden_in)
    increment = product(weight_in.T, back_in)
    bias_part = product(residual_term, pred_rows.T)
    return model_out, increment, bias_part


def reference(model_state, obs_cell, obs_count, obs_value, obs_weight, predictor, bias_coef, weight_in, bias_in, weight_mid, bias_mid, weight_out, bias_out):
    features = model_state.shape[0]
    flat_state = model_state.reshape(features, NX * NY)
    position = jnp.arange(OBS_DEV, dtype=jnp.int32)
    source = position // CAP
    base_row = (source // N_GY) * CX
    base_col = (source % N_GY) * CY
    global_cell = ((base_row[None, :] + obs_cell // CY) * NY + base_col[None, :] + obs_cell % CY).astype(jnp.int32)
    valid_slot = (jnp.arange(CAP, dtype=jnp.int32)[None, None, :] < obs_count[:, :, None]).reshape(DEVICES, OBS_DEV)
    value_blocks = obs_value.reshape(CH, DEVICES, OBS_DEV).transpose(1, 0, 2)
    weight_blocks = jnp.where(valid_slot[:, None, :], obs_weight.reshape(CH, DEVICES, OBS_DEV).transpose(1, 0, 2), jnp.float32(0.0))
    pred_blocks = predictor.reshape(NPRED, DEVICES, OBS_DEV).transpose(1, 0, 2)

    def owner_step(owner_items):
        cell_index, obs_rows, weight_rows, pred_rows = owner_items
        profile = jnp.take(flat_state, cell_index, axis=1)
        return observe(profile, obs_rows, weight_rows, pred_rows, bias_coef, weight_in, bias_in, weight_mid, bias_mid, weight_out, bias_out)

    model_out, increment, bias_part = lax.map(owner_step, (global_cell, value_blocks, weight_blocks, pred_blocks))
    evolved = jnp.where(valid_slot[:, None, :], model_out, jnp.float32(0.0)).transpose(1, 0, 2).reshape(CH, DEVICES * OBS_DEV)
    spread_back = increment.transpose(1, 0, 2).reshape(features, DEVICES * OBS_DEV)
    gradient = jnp.zeros((features, NX * NY), jnp.float32).at[:, global_cell.reshape(-1)].add(spread_back)
    return gradient.reshape(features, NX, NY), evolved, jnp.sum(bias_part, axis=0)
```

```python
import functools

import jax
import jax.numpy as jnp
from jax import lax
from jax.experimental import pallas as pl
from jax.experimental.pallas import tpu as pltpu
from jax.sharding import PartitionSpec as P

F32 = jnp.float32
BF16 = jnp.bfloat16
LANES = 128
GROUP = 16
TILE = 512


def split(x):
    high = x.astype(BF16)
    return high, (x - high.astype(F32)).astype(BF16)


def mm(lhs, rhs):
    return jnp.dot(lhs, rhs, preferred_element_type=F32)


def mm3(lhs, rhs_high, rhs_low):
    high, low = split(lhs)
    return mm(high, rhs_high) + (mm(low, rhs_high) + mm(high, rhs_low))


def swap_groups(x):
    rows = x.shape[0]
    differ = lax.broadcasted_iota(jnp.int32, x.shape, 0) ^ (
        lax.broadcasted_iota(jnp.int32, x.shape, 1) // GROUP
    )
    group = lax.broadcasted_iota(jnp.int32, x.shape, 1) // GROUP
    for bit in (1, 2, 4):
        up = pltpu.roll(pltpu.roll(x, rows - bit, 0), GROUP * bit, 1)
        down = pltpu.roll(pltpu.roll(x, bit, 0), LANES - GROUP * bit, 1)
        moved = jnp.where((group & bit) != 0, up, down)
        x = jnp.where((differ & bit) == 0, x, moved)
    return x


def to_tiles(arrays):
    return jnp.concatenate(
        [a[:, i : i + LANES] for a in arrays for i in range(0, a.shape[1], LANES)], axis=0
    )


def used_slots(count_ref):
    peers = count_ref.shape[1]
    counts = jnp.broadcast_to(count_ref[...].astype(F32), (peers, peers)).T
    slot = lax.broadcasted_iota(jnp.int32, (peers, LANES), 1) % GROUP
    return slot.astype(F32) < counts


def request_kernel(cell, count, obs, weight, pred, coef, bias, send, base):
    peers = count.shape[1]
    linear = jnp.broadcast_to(bias[...], obs.shape)
    for i in range(pred.shape[0]):
        linear = linear + coef[:, i : i + 1] * pred[i : i + 1, :]
    base[...] = linear
    target = obs[...] - linear
    cells = jnp.broadcast_to(cell[...].astype(F32), (8, cell.shape[1]))
    packed = swap_groups(
        to_tiles([target[:8], target[8:], weight[:8, :], weight[8:, :], pred[...], cells])
    )
    used = used_slots(count)
    for a in range(6):
        rows = packed[a * peers : (a + 1) * peers]
        if a in (2, 3):
            rows = jnp.where(used, rows, 0.0)
        send[pl.ds(a, peers, stride=8), :] = rows


def prepare_kernel(state, w_in_t, w_mid, w_out, s0, s1, wi_f, wi_b, wm_f, wm_b, wo_f, wo_b):
    feat, rows, cols = 200, 32, 128
    hid = w_mid.shape[0]
    fill = jnp.zeros((256 - feat, cols), F32)
    for r in range(rows):
        block = jnp.concatenate([state[pl.ds(r, feat, stride=rows), :], fill], axis=0)
        turned = block.T
        s0[r * cols : (r + 1) * cols, :] = turned[:, :128]
        s1[r * cols : (r + 1) * cols, :] = turned[:, 128:]
    w_in = jnp.concatenate([w_in_t[...], jnp.zeros((256 - feat, hid), F32)], axis=0)
    wi_f[0], wi_f[1] = split(w_in)
    wi_b[0], wi_b[1] = split(w_in.T)
    wm_b[0], wm_b[1] = split(w_mid[...])
    wm_f[0], wm_f[1] = split(w_mid[...].T)
    out_high, out_low = split(w_out[...])
    out_high = out_high.astype(F32)
    out_low = out_low.astype(F32)
    chan = w_out.shape[0]
    stack = jnp.concatenate([out_high, out_low, jnp.zeros((128 - 2 * chan, hid), F32)], axis=0)
    wo_f[...] = stack.T.astype(BF16)
    wo_b[...] = jnp.concatenate(
        [out_high, out_low, out_high, jnp.zeros((128 - 3 * chan, hid), F32)], axis=0
    ).astype(BF16)


def forward_kernel(
    recv, s0, s1, wi, wm, wo, b_in, b_mid,
    h1_out, h2_out, r_out, cell_out, send,
    g0, g1, q, w, p, z, moments, cell_smem, sem,
):
    step = pl.program_id(0)
    peers = recv.shape[0] // 8
    blocks = peers // 8

    @pl.when(step == 0)
    def _():
        packed = jnp.concatenate([recv[pl.ds(a, peers, stride=8), :] for a in range(6)], axis=0)
        tiles = swap_groups(packed)
        for i in range(blocks):
            lanes = slice(i * LANES, (i + 1) * LANES)

            def tile(a, i=i):
                return tiles[(a * blocks + i) * 8 : (a * blocks + i) * 8 + 8]

            q[0:8, lanes] = tile(0)
            q[8:16, lanes] = tile(1)
            w[0:8, lanes] = tile(2)
            w[8:16, lanes] = tile(3)
            p[:, lanes] = tile(4)
            cell_out[i : i + 1, :] = tile(5)[0:1].astype(jnp.int32)
        copy = pltpu.make_async_copy(cell_out, cell_smem, sem)
        copy.start()
        moments[...] = jnp.zeros_like(moments)
        copy.wait()

        def gather(i, carry):
            for k in range(GROUP):
                n = i * GROUP + k
                c = cell_smem[i // 8, (i % 8) * GROUP + k]
                g0[pl.ds(n, 1), :] = s0[pl.ds(c, 1), :]
                g1[pl.ds(n, 1), :] = s1[pl.ds(c, 1), :]
            return carry

        lax.fori_loop(0, peers, gather, 0)

    start = pl.multiple_of(step * TILE, TILE)
    here = pl.ds(start, TILE)
    profile = jnp.concatenate([g0[here, :], g1[here, :]], axis=1)
    h1 = jnp.tanh(mm3(profile, wi[0], wi[1]) + b_in[...])
    h1_out[...] = h1
    h2 = jnp.tanh(mm3(h1, wm[0], wm[1]) + b_mid[...])
    h2_out[...] = h2
    high, low = split(h2)
    total = (mm(high, wo[...]) + mm(low, wo[...])).T
    zt = total[0:16] + total[16:32]
    z[:, here] = zt
    residual = w[:, here] * (zt - q[:, here])
    moments[...] += lax.dot_general(
        p[:, here], jnp.concatenate([residual] * 8, axis=0),
        (((1,), (1,)), ((), ())), precision=lax.Precision.HIGHEST, preferred_element_type=F32,
    )
    r_high, r_low = split(residual)
    r_high = r_high.astype(F32)
    r_stack = jnp.concatenate(
        [r_high, r_high, r_low.astype(F32), jnp.zeros((LANES - 48, TILE), F32)], axis=0
    )
    r_out[...] = r_stack.T.astype(BF16)

    @pl.when(step == pl.num_programs(0) - 1)
    def _():
        packed = swap_groups(to_tiles([z[0:8, :], z[8:16, :]]))
        send[pl.ds(0, peers, stride=8), :] = packed[:peers]
        send[pl.ds(1, peers, stride=8), :] = packed[peers:]
        lane_group = lax.broadcasted_iota(jnp.int32, (8, LANES), 1) // GROUP
        own = lane_group == lax.broadcasted_iota(jnp.int32, (8, LANES), 0)
        row = jnp.sum(jnp.where(own, moments[...], 0.0), axis=0, keepdims=True)
        send[pl.ds(2, peers, stride=8), :] = jnp.broadcast_to(row, (peers, LANES))


def backward_kernel(cells, h1, h2, r, wo, wm, wi, grad, i0, i1, a0, a1, c0, c1):
    step = pl.program_id(0)

    @pl.when(step == 0)
    def _():
        for acc in (a0, a1, c0, c1):
            acc[...] = jnp.zeros_like(acc)

    x2 = h2[...]
    back_mid = mm(r[...], wo[...]) * (1.0 - x2 * x2)
    x1 = h1[...]
    back_in = mm3(back_mid, wm[0], wm[1]) * (1.0 - x1 * x1)
    inc = mm3(back_in, wi[0], wi[1])
    i0[...] = inc[:, :128]
    i1[...] = inc[:, 128:]

    def scatter(i, carry):
        for k in range(0, GROUP, 2):
            n = i * GROUP + k
            g = step * (TILE // GROUP) + i
            ca = cells[g // 8, (g % 8) * GROUP + k]
            cb = cells[g // 8, (g % 8) * GROUP + k + 1]
            a0[pl.ds(ca, 1), :] += i0[pl.ds(n, 1), :]
            a1[pl.ds(ca, 1), :] += i1[pl.ds(n, 1), :]
            c0[pl.ds(cb, 1), :] += i0[pl.ds(n + 1, 1), :]
            c1[pl.ds(cb, 1), :] += i1[pl.ds(n + 1, 1), :]
        return carry

    lax.fori_loop(0, TILE // GROUP, scatter, 0)

    @pl.when(step == pl.num_programs(0) - 1)
    def _():
        rows, cols, feat = 32, 128, 200
        for row in range(rows):
            at = slice(row * cols, (row + 1) * cols)
            block = jnp.concatenate([a0[at, :] + c0[at, :], a1[at, :] + c1[at, :]], axis=1)
            grad[pl.ds(row, feat, stride=rows), :] = block.T[:feat]


def finish_kernel(recv, base, count, evolved, bias_grad):
    peers = count.shape[1]
    used = jnp.where(used_slots(count), 1.0, 0.0)
    tiles = swap_groups(
        jnp.concatenate(
            [recv[pl.ds(0, peers, stride=8), :], recv[pl.ds(1, peers, stride=8), :], used], axis=0
        )
    )
    blocks = peers // 8
    for i in range(blocks):
        lanes = slice(i * LANES, (i + 1) * LANES)
        keep = tiles[(2 * blocks + i) * 8 : (2 * blocks + i) * 8 + 8] > 0.5
        for a in range(2):
            value = tiles[(a * blocks + i) * 8 : (a * blocks + i) * 8 + 8]
            rows = slice(8 * a, 8 * a + 8)
            evolved[rows, lanes] = jnp.where(keep, value + base[rows, lanes], 0.0)
    row = jnp.sum(recv[pl.ds(2, peers, stride=8), :], axis=0, keepdims=True)
    lane = lax.broadcasted_iota(jnp.int32, (16, LANES), 1)
    chan = lax.broadcasted_iota(jnp.int32, (16, LANES), 0)
    spread = jnp.where(lane % GROUP == chan, jnp.broadcast_to(row, (16, LANES)), 0.0)
    pick = lax.broadcasted_iota(jnp.int32, (LANES, 8), 0) // GROUP == lax.broadcasted_iota(
        jnp.int32, (LANES, 8), 1
    )
    bias_grad[...] = jnp.dot(
        spread, jnp.where(pick, 1.0, 0.0), precision=lax.Precision.HIGHEST,
        preferred_element_type=F32,
    )


def shape(dims, dtype=F32):
    return jax.ShapeDtypeStruct(dims, dtype)


def exchange(data, peers):
    blocks = data.reshape(peers, 8, LANES)
    blocks = lax.all_to_all(blocks, ("gx", "gy"), split_axis=0, concat_axis=0, tiled=True)
    return blocks.reshape(peers * 8, LANES)


def per_device(
    model_state, obs_cell, obs_count, obs_value, obs_weight, predictor, bias_coef,
    weight_in, bias_in, weight_mid, bias_mid, weight_out, bias_out,
):
    feat, rows, cols = model_state.shape
    slots = obs_cell.shape[1]
    peers = obs_count.shape[1]
    hid = weight_mid.shape[0]
    cells = rows * cols
    send, base = pl.pallas_call(
        request_kernel,
        out_shape=(shape((peers * 8, LANES)), shape((16, slots))),
        name="request",
    )(obs_cell, obs_count, obs_value, obs_weight, predictor, bias_coef, bias_out[:, None])
    recv = exchange(send, peers)
    s0, s1, wi_f, wi_b, wm_f, wm_b, wo_f, wo_b = pl.pallas_call(
        prepare_kernel,
        out_shape=(
            shape((cells, 128)), shape((cells, 128)),
            shape((2, 256, hid), BF16), shape((2, hid, 256), BF16),
            shape((2, hid, hid), BF16), shape((2, hid, hid), BF16),
            shape((hid, 128), BF16), shape((128, hid), BF16),
        ),
        name="prepare",
        cost_estimate=pl.CostEstimate(flops=10**7, transcendentals=0, bytes_accessed=15 * 10**6),
    )(model_state.reshape(feat * rows, cols), weight_in.T, weight_mid, weight_out)

    def whole(dims):
        return pl.BlockSpec(dims, lambda i: (0,) * len(dims))

    steps = slots // TILE
    h1, h2, residual, cell, reply = pl.pallas_call(
        forward_kernel,
        grid=(steps,),
        in_specs=[
            whole((peers * 8, LANES)), whole((cells, 128)), whole((cells, 128)),
            whole((2, 256, hid)), whole((2, hid, hid)), whole((hid, 128)),
            whole((1, hid)), whole((1, hid)),
        ],
        out_specs=[
            pl.BlockSpec((TILE, hid), lambda i: (i, 0)),
            pl.BlockSpec((TILE, hid), lambda i: (i, 0)),
            pl.BlockSpec((TILE, 128), lambda i: (i, 0)),
            whole((slots // LANES, LANES)),
            whole((peers * 8, LANES)),
        ],
        out_shape=(
            shape((slots, hid)), shape((slots, hid)), shape((slots, 128), BF16),
            shape((slots // LANES, LANES), jnp.int32), shape((peers * 8, LANES)),
        ),
        scratch_shapes=[
            pltpu.VMEM((slots, 128), F32), pltpu.VMEM((slots, 128), F32),
            pltpu.VMEM((16, slots), F32), pltpu.VMEM((16, slots), F32),
            pltpu.VMEM((8, slots), F32), pltpu.VMEM((16, slots), F32),
            pltpu.VMEM((8, LANES), F32),
            pltpu.SMEM((slots // LANES, LANES), jnp.int32),
            pltpu.SemaphoreType.DMA(()),
        ],
        name="forward",
        cost_estimate=pl.CostEstimate(
            flops=6 * slots * hid * (256 + hid + 128), transcendentals=2 * slots * hid,
            bytes_accessed=25 * 10**6,
        ),
    )(recv, s0, s1, wi_f, wm_f, wo_f, bias_in[None, :], bias_mid[None, :])
    back = exchange(reply, peers)
    gradient = pl.pallas_call(
        backward_kernel,
        grid=(steps,),
        in_specs=[
            pl.BlockSpec(memory_space=pltpu.SMEM),
            pl.BlockSpec((TILE, hid), lambda i: (i, 0)),
            pl.BlockSpec((TILE, hid), lambda i: (i, 0)),
            pl.BlockSpec((TILE, 128), lambda i: (i, 0)),
            whole((128, hid)), whole((2, hid, hid)), whole((2, hid, 256)),
        ],
        out_specs=whole((feat * rows, cols)),
        out_shape=shape((feat * rows, cols)),
        scratch_shapes=[pltpu.VMEM((TILE, 128), F32), pltpu.VMEM((TILE, 128), F32)]
        + [pltpu.VMEM((cells, 128), F32) for _ in range(4)],
        name="backward",
        cost_estimate=pl.CostEstimate(
            flops=6 * slots * hid * (256 + hid + 128), transcendentals=0,
            bytes_accessed=25 * 10**6,
        ),
    )(cell, h1, h2, residual, wo_b, wm_b, wi_b)
    evolved, bias_gradient = pl.pallas_call(
        finish_kernel,
        out_shape=(shape((16, slots)), shape((16, 8))),
        name="finish",
    )(back, base, obs_count)
    return gradient.reshape(feat, rows, cols), evolved, bias_gradient


def solution(mesh):
    in_specs = (
        P(None, "gx", "gy"),
        P(("gx", "gy"), None),
        P(("gx", "gy"), None),
        P(None, ("gx", "gy")),
        P(None, ("gx", "gy")),
        P(None, ("gx", "gy")),
        P(),
        P(),
        P(),
        P(),
        P(),
        P(),
        P(),
    )
    out_specs = (P(None, "gx", "gy"), P(None, ("gx", "gy")), P())
    return jax.shard_map(
        per_device, mesh=mesh, in_specs=in_specs, out_specs=out_specs, check_vma=False
    )
```

```python
import jax
import jax.numpy as jnp
from jax import lax
from jax.experimental import pallas as pl
from jax.experimental.pallas import tpu as pltpu
from jax.sharding import PartitionSpec as P

F32 = jnp.float32
BF16 = jnp.bfloat16
LANES = 128
GROUP = 16
TILE = 512


def split(x):
    high = x.astype(BF16)
    return high, (x - high.astype(F32)).astype(BF16)


def mm(lhs, rhs):
    return jnp.dot(lhs, rhs, preferred_element_type=F32)


def mm3_of(high, low, rhs_high, rhs_low):
    return mm(
        jnp.concatenate([high, low, high], axis=1),
        jnp.concatenate([rhs_high, rhs_high, rhs_low], axis=0),
    )


def mm3(lhs, rhs_high, rhs_low):
    return mm3_of(*split(lhs), rhs_high, rhs_low)


def swap_groups(x):
    rows = x.shape[0]
    differ = lax.broadcasted_iota(jnp.int32, x.shape, 0) ^ (
        lax.broadcasted_iota(jnp.int32, x.shape, 1) // GROUP
    )
    group = lax.broadcasted_iota(jnp.int32, x.shape, 1) // GROUP
    for bit in (1, 2, 4):
        up = pltpu.roll(pltpu.roll(x, rows - bit, 0), GROUP * bit, 1)
        down = pltpu.roll(pltpu.roll(x, bit, 0), LANES - GROUP * bit, 1)
        moved = jnp.where((group & bit) != 0, up, down)
        x = jnp.where((differ & bit) == 0, x, moved)
    return x


def to_tiles(arrays):
    return jnp.concatenate(
        [a[:, i : i + LANES] for a in arrays for i in range(0, a.shape[1], LANES)], axis=0
    )


def used_slots(count_ref):
    peers = count_ref.shape[1]
    counts = jnp.broadcast_to(count_ref[...].astype(F32), (peers, peers)).T
    slot = lax.broadcasted_iota(jnp.int32, (peers, LANES), 1) % GROUP
    return slot.astype(F32) < counts


def request_kernel(cell, count, obs, weight, pred, coef_t, bias, send, base):
    peers = count.shape[1]
    coef = jnp.concatenate([coef_t[...], jnp.broadcast_to(bias[...], coef_t.shape)], axis=0).T
    preds = pred.shape[0]
    linear = jnp.broadcast_to(coef[:, preds : preds + 1], obs.shape)
    for i in range(preds):
        linear = linear + coef[:, i : i + 1] * pred[i : i + 1, :]
    base[...] = linear
    target = obs[...] - linear
    cells = jnp.broadcast_to(cell[...].astype(F32), (8, cell.shape[1]))
    packed = swap_groups(
        to_tiles([target[:8], target[8:], weight[:8, :], weight[8:, :], pred[...], cells])
    )
    used = used_slots(count)
    for a in range(6):
        rows = packed[a * peers : (a + 1) * peers]
        if a in (2, 3):
            rows = jnp.where(used, rows, 0.0)
        send[pl.ds(a, peers, stride=8), :] = rows


def prepare_kernel(state, w_in_t, w_mid, w_out, s0, s1, wi_f, wi_b, wm_f, wm_b, wo_f, wo_b):
    feat, rows, cols = 200, 32, 128
    hid = w_mid.shape[0]
    fill = jnp.zeros((256 - feat, cols), F32)
    for r in range(rows):
        block = jnp.concatenate([state[pl.ds(r, feat, stride=rows), :], fill], axis=0)
        turned = block.T
        s0[r * cols : (r + 1) * cols, :] = turned[:, :128]
        s1[r * cols : (r + 1) * cols, :] = turned[:, 128:]
    w_in = jnp.concatenate([w_in_t[...], jnp.zeros((256 - feat, hid), F32)], axis=0)
    wi_f[0], wi_f[1] = split(w_in)
    wi_b[0], wi_b[1] = split(w_in.T)
    wm_b[0], wm_b[1] = split(w_mid[...])
    wm_f[0], wm_f[1] = split(w_mid[...].T)
    out_high, out_low = split(w_out[...])
    out_high = out_high.astype(F32)
    out_low = out_low.astype(F32)
    chan = w_out.shape[0]
    stack = jnp.concatenate([out_high, out_low, jnp.zeros((128 - 2 * chan, hid), F32)], axis=0)
    wo_f[...] = stack.T.astype(BF16)
    wo_b[...] = jnp.concatenate(
        [out_high, out_low, out_high, jnp.zeros((128 - 3 * chan, hid), F32)], axis=0
    ).astype(BF16)


def forward_kernel(
    recv, s0_hbm, s1_hbm, wi_hbm, wm_hbm, wo_hbm, b_in, b_mid,
    h1_out, h2_out, r_out, cell_out, send,
    s0, s1, wi, wm, wo, g0, g1, q, w, p, z, moments, cell_smem, sems,
):
    step = pl.program_id(0)
    peers = recv.shape[0] // 8
    blocks = peers // 8

    def fetch(row, to_row):
        g0[pl.ds(to_row, 1), :] = s0[pl.ds(row, 1), :]
        g1[pl.ds(to_row, 1), :] = s1[pl.ds(row, 1), :]

    @pl.when(step == 0)
    def _():
        copies = [
            pltpu.make_async_copy(source, target, sems.at[i])
            for i, (source, target) in enumerate(
                ((s0_hbm, s0), (s1_hbm, s1), (wi_hbm, wi), (wm_hbm, wm), (wo_hbm, wo))
            )
        ]
        for copy in copies:
            copy.start()
        packed = jnp.concatenate([recv[pl.ds(a, peers, stride=8), :] for a in range(6)], axis=0)
        tiles = swap_groups(packed)

        def tile(a, i):
            return tiles[(a * blocks + i) * 8 : (a * blocks + i) * 8 + 8]

        for i in range(blocks):
            cell_out[i : i + 1, :] = tile(5, i)[0:1].astype(jnp.int32)
        copy = pltpu.make_async_copy(cell_out, cell_smem, sems.at[5])
        copy.start()
        for i in range(blocks):
            lanes = slice(i * LANES, (i + 1) * LANES)
            q[0:8, lanes] = tile(0, i)
            q[8:16, lanes] = tile(1, i)
            w[0:8, lanes] = tile(2, i)
            w[8:16, lanes] = tile(3, i)
            p[:, lanes] = tile(4, i)
        moments[...] = jnp.zeros_like(moments)
        copy.wait()
        copies[0].wait()
        copies[1].wait()

        def gather(i, carry):
            for k in range(GROUP):
                fetch(cell_smem[i // 8, (i % 8) * GROUP + k], i * GROUP + k)
            return carry

        lax.fori_loop(0, TILE // GROUP, gather, 0)
        for copy in copies[2:]:
            copy.wait()

    start = pl.multiple_of(step * TILE, TILE)
    here = pl.ds(start, TILE)
    high, low = split(jnp.concatenate([g0[here, :], g1[here, :]], axis=1))
    following = jnp.minimum(step + 1, pl.num_programs(0) - 1)
    for n in range(TILE):
        fetch(
            cell_smem[following * (TILE // LANES) + n // LANES, n % LANES], following * TILE + n
        )
    h1 = jnp.tanh(mm3_of(high, low, wi[0], wi[1]) + b_in[...][None, :])
    h1_out[...] = h1
    h2 = jnp.tanh(mm3(h1, wm[0], wm[1]) + b_mid[...][None, :])
    h2_out[...] = h2
    high, low = split(h2)
    total = (mm(high, wo[...]) + mm(low, wo[...])).T
    zt = total[0:16] + total[16:32]
    z[:, here] = zt
    residual = w[:, here] * (zt - q[:, here])
    moments[...] += lax.dot_general(
        p[:, here], jnp.concatenate([residual] * 8, axis=0),
        (((1,), (1,)), ((), ())), precision=lax.Precision.HIGHEST, preferred_element_type=F32,
    )
    r_high, r_low = split(residual)
    r_high = r_high.astype(F32)
    r_stack = jnp.concatenate(
        [r_high, r_high, r_low.astype(F32), jnp.zeros((LANES - 48, TILE), F32)], axis=0
    )
    r_out[...] = r_stack.T.astype(BF16)

    @pl.when(step == pl.num_programs(0) - 1)
    def _():
        packed = swap_groups(to_tiles([z[0:8, :], z[8:16, :]]))
        send[pl.ds(0, peers, stride=8), :] = packed[:peers]
        send[pl.ds(1, peers, stride=8), :] = packed[peers:]
        lane_group = lax.broadcasted_iota(jnp.int32, (8, LANES), 1) // GROUP
        own = lane_group == lax.broadcasted_iota(jnp.int32, (8, LANES), 0)
        row = jnp.sum(jnp.where(own, moments[...], 0.0), axis=0, keepdims=True)
        send[pl.ds(2, peers, stride=8), :] = jnp.broadcast_to(row, (peers, LANES))


def backward_kernel(
    cells, h1_hbm, h2_hbm, r, wo_hbm, wm_hbm, wi_hbm, grad,
    h1, h2, wo, wm, wi, i0, i1, a0, a1, c0, c1, out, sems, h1_sems, h2_sems, out_sems,
):
    step = pl.program_id(0)
    last = pl.num_programs(0) - 1
    steps = h1.shape[0] // TILE

    def tile_copy(source, target, some_sems, i):
        rows = pl.ds(pl.multiple_of(i * TILE, TILE), TILE)
        return pltpu.make_async_copy(source.at[rows, :], target.at[rows, :], some_sems.at[i])

    @pl.when(step == 0)
    def _():
        weights = [
            pltpu.make_async_copy(source, target, sems.at[i])
            for i, (source, target) in enumerate(((wo_hbm, wo), (wm_hbm, wm), (wi_hbm, wi)))
        ]
        weights[0].start()
        tile_copy(h2_hbm, h2, h2_sems, 0).start()
        weights[1].start()
        tile_copy(h1_hbm, h1, h1_sems, 0).start()
        weights[2].start()
        for i in range(1, steps):
            tile_copy(h2_hbm, h2, h2_sems, i).start()
            tile_copy(h1_hbm, h1, h1_sems, i).start()
        for acc in (a0, a1, c0, c1, i0, i1):
            acc[...] = jnp.zeros_like(acc)
        for copy in weights:
            copy.wait()

    tile_copy(h2_hbm, h2, h2_sems, step).wait()
    tile_copy(h1_hbm, h1, h1_sems, step).wait()
    start = pl.multiple_of(step * TILE, TILE)

    def add(first, second, n):
        a0[pl.ds(first, 1), :] += i0[pl.ds(n, 1), :]
        a1[pl.ds(first, 1), :] += i1[pl.ds(n, 1), :]
        c0[pl.ds(second, 1), :] += i0[pl.ds(n + 1, 1), :]
        c1[pl.ds(second, 1), :] += i1[pl.ds(n + 1, 1), :]

    before = jnp.maximum(step - 1, 0) * (TILE // LANES)
    for n in range(0, TILE, 2):
        row = before + n // LANES
        add(cells[row, n % LANES], cells[row, n % LANES + 1], n)
    halves = [slice(0, TILE // 2), slice(TILE // 2, TILE)]
    mids = []
    for s in halves:
        x2 = h2[pl.ds(start + s.start, TILE // 2), :]
        mids.append(mm(r[s, :], wo[...]) * (1.0 - x2 * x2))
    ins = []
    for s, back_mid in zip(halves, mids):
        x1 = h1[pl.ds(start + s.start, TILE // 2), :]
        ins.append(mm3(back_mid, wm[0], wm[1]) * (1.0 - x1 * x1))
    for s, back_in in zip(halves, ins):
        increment = mm3(back_in, wi[0], wi[1])
        i0[s, :] = increment[:, :128]
        i1[s, :] = increment[:, 128:]

    @pl.when(step == last)
    def _():
        def scatter(i, carry):
            row = last * (TILE // LANES) + i // 8
            for k in range(0, GROUP, 2):
                at = (i % 8) * GROUP + k
                add(cells[row, at], cells[row, at + 1], i * GROUP + k)
            return carry

        lax.fori_loop(0, TILE // GROUP, scatter, 0)
        feat, rows, cols = grad.shape
        copies = []
        for row in range(rows):
            at = slice(row * cols, (row + 1) * cols)
            block = jnp.concatenate([a0[at, :] + c0[at, :], a1[at, :] + c1[at, :]], axis=1)
            out[row] = block.T[:feat]
            copies.append(pltpu.make_async_copy(out.at[row], grad.at[:, row, :], out_sems.at[row]))
            copies[-1].start()
        for copy in copies:
            copy.wait()


def finish_kernel(recv, base, count, evolved, bias_grad):
    peers = count.shape[1]
    used = jnp.where(used_slots(count), 1.0, 0.0)
    tiles = swap_groups(
        jnp.concatenate(
            [recv[pl.ds(0, peers, stride=8), :], recv[pl.ds(1, peers, stride=8), :], used], axis=0
        )
    )
    blocks = peers // 8
    for i in range(blocks):
        lanes = slice(i * LANES, (i + 1) * LANES)
        keep = tiles[(2 * blocks + i) * 8 : (2 * blocks + i) * 8 + 8] > 0.5
        for a in range(2):
            value = tiles[(a * blocks + i) * 8 : (a * blocks + i) * 8 + 8]
            rows = slice(8 * a, 8 * a + 8)
            evolved[rows, lanes] = jnp.where(keep, value + base[rows, lanes], 0.0)
    row = jnp.sum(recv[pl.ds(2, peers, stride=8), :], axis=0, keepdims=True)
    lane = lax.broadcasted_iota(jnp.int32, (8, LANES), 1)
    spread = jnp.where(
        lane // GROUP == lax.broadcasted_iota(jnp.int32, (8, LANES), 0),
        jnp.broadcast_to(row, (8, LANES)), 0.0,
    )
    pick = lax.broadcasted_iota(jnp.int32, (LANES, 16), 0) % GROUP == lax.broadcasted_iota(
        jnp.int32, (LANES, 16), 1
    )
    bias_grad[...] = jnp.dot(
        spread, jnp.where(pick, 1.0, 0.0), precision=lax.Precision.HIGHEST,
        preferred_element_type=F32,
    )


def limit(mebibytes):
    return pltpu.CompilerParams(vmem_limit_bytes=mebibytes * 2**20)


def stay(x):
    return pltpu.with_memory_space_constraint(x, pltpu.HBM)


def shape(dims, dtype=F32):
    return pltpu.HBM(dims, dtype)


def exchange(data, peers):
    blocks = data.reshape(peers, 8, LANES)
    blocks = lax.all_to_all(blocks, ("gx", "gy"), split_axis=0, concat_axis=0, tiled=True)
    return blocks.reshape(peers * 8, LANES)


def per_device(
    model_state, obs_cell, obs_count, obs_value, obs_weight, predictor, bias_coef,
    weight_in, bias_in, weight_mid, bias_mid, weight_out, bias_out,
):
    feat, rows, cols = model_state.shape
    slots = obs_cell.shape[1]
    peers = obs_count.shape[1]
    hid = weight_mid.shape[0]
    cells = rows * cols
    send, base = pl.pallas_call(
        request_kernel,
        out_shape=(shape((peers * 8, LANES)), shape((16, slots))),
        name="request",
    )(obs_cell, obs_count, obs_value, obs_weight, predictor, bias_coef.T, bias_out[None, :])
    recv = exchange(send, peers)
    s0, s1, wi_f, wi_b, wm_f, wm_b, wo_f, wo_b = pl.pallas_call(
        prepare_kernel,
        out_shape=(
            shape((cells, 128)), shape((cells, 128)),
            shape((2, 256, hid), BF16), shape((2, hid, 256), BF16),
            shape((2, hid, hid), BF16), shape((2, hid, hid), BF16),
            shape((hid, 128), BF16), shape((128, hid), BF16),
        ),
        name="prepare",
        cost_estimate=pl.CostEstimate(flops=10**7, transcendentals=0, bytes_accessed=15 * 10**6),
    )(model_state.reshape(feat * rows, cols), weight_in.T, weight_mid, weight_out)

    def whole(dims):
        return pl.BlockSpec(dims, lambda i: (0,) * len(dims))

    steps = slots // TILE
    in_hbm = pl.BlockSpec(memory_space=pltpu.HBM)
    h1, h2, residual, cell, reply = pl.pallas_call(
        forward_kernel,
        grid=(steps,),
        in_specs=[
            whole((peers * 8, LANES)), in_hbm, in_hbm, in_hbm, in_hbm, in_hbm,
            whole((hid,)), whole((hid,)),
        ],
        out_specs=[
            pl.BlockSpec((TILE, hid), lambda i: (i, 0)),
            pl.BlockSpec((TILE, hid), lambda i: (i, 0)),
            pl.BlockSpec((TILE, 128), lambda i: (i, 0)),
            whole((slots // LANES, LANES)),
            whole((peers * 8, LANES)),
        ],
        out_shape=(
            shape((slots, hid)), shape((slots, hid)), shape((slots, 128), BF16),
            shape((slots // LANES, LANES), jnp.int32), shape((peers * 8, LANES)),
        ),
        scratch_shapes=[
            pltpu.VMEM((cells, 128), F32), pltpu.VMEM((cells, 128), F32),
            pltpu.VMEM((2, 256, hid), BF16), pltpu.VMEM((2, hid, hid), BF16),
            pltpu.VMEM((hid, 128), BF16),
            pltpu.VMEM((slots, 128), F32), pltpu.VMEM((slots, 128), F32),
            pltpu.VMEM((16, slots), F32), pltpu.VMEM((16, slots), F32),
            pltpu.VMEM((8, slots), F32), pltpu.VMEM((16, slots), F32),
            pltpu.VMEM((8, LANES), F32),
            pltpu.SMEM((slots // LANES, LANES), jnp.int32),
            pltpu.SemaphoreType.DMA((6,)),
        ],
        name="forward",
        compiler_params=limit(48),
        cost_estimate=pl.CostEstimate(
            flops=6 * slots * hid * (256 + hid + 128), transcendentals=2 * slots * hid,
            bytes_accessed=25 * 10**6,
        ),
    )(recv, *map(stay, (s0, s1, wi_f, wm_f, wo_f)), bias_in, bias_mid)
    back = exchange(reply, peers)
    gradient = pl.pallas_call(
        backward_kernel,
        grid=(steps,),
        in_specs=[
            pl.BlockSpec(memory_space=pltpu.SMEM),
            in_hbm, in_hbm,
            pl.BlockSpec((TILE, 128), lambda i: (i, 0)),
            in_hbm, in_hbm, in_hbm,
        ],
        out_specs=in_hbm,
        out_shape=shape((feat, rows, cols)),
        scratch_shapes=[
            pltpu.VMEM((slots, hid), F32), pltpu.VMEM((slots, hid), F32),
            pltpu.VMEM((128, hid), BF16), pltpu.VMEM((2, hid, hid), BF16),
            pltpu.VMEM((2, hid, 256), BF16),
            pltpu.VMEM((TILE, 128), F32), pltpu.VMEM((TILE, 128), F32),
        ]
        + [pltpu.VMEM((cells, 128), F32) for _ in range(4)]
        + [
            pltpu.VMEM((rows, feat, cols), F32),
            pltpu.SemaphoreType.DMA((3,)), pltpu.SemaphoreType.DMA((steps,)),
            pltpu.SemaphoreType.DMA((steps,)), pltpu.SemaphoreType.DMA((rows,)),
        ],
        name="backward",
        cost_estimate=pl.CostEstimate(
            flops=6 * slots * hid * (256 + hid + 128), transcendentals=0,
            bytes_accessed=25 * 10**6,
        ),
    )(cell, h1, h2, residual, wo_b, wm_b, wi_b)
    evolved, bias_gradient = pl.pallas_call(
        finish_kernel,
        out_shape=(shape((16, slots)), shape((8, 16))),
        name="finish",
        compiler_params=limit(8),
    )(back, base, obs_count)
    return gradient, evolved, bias_gradient.T


def solution(mesh):
    in_specs = (
        P(None, "gx", "gy"),
        P(("gx", "gy"), None),
        P(("gx", "gy"), None),
        P(None, ("gx", "gy")),
        P(None, ("gx", "gy")),
        P(None, ("gx", "gy")),
        P(),
        P(),
        P(),
        P(),
        P(),
        P(),
        P(),
    )
    out_specs = (P(None, "gx", "gy"), P(None, ("gx", "gy")), P())
    return jax.shard_map(
        per_device, mesh=mesh, in_specs=in_specs, out_specs=out_specs, check_vma=False
    )
```

```python
import jax
import jax.numpy as jnp
from jax import lax
from jax.experimental import pallas as pl
from jax.experimental.pallas import tpu as pltpu
from jax.sharding import PartitionSpec as P

F32 = jnp.float32
BF16 = jnp.bfloat16
LANES = 128
GROUP = 16
TILE = 512
ASK = 6
REPLY = 3


def split(x):
    high = x.astype(BF16)
    return high, (x - high.astype(F32)).astype(BF16)


def mm(lhs, rhs):
    return jnp.dot(lhs, rhs, preferred_element_type=F32)


def mm3(parts, rhs):
    high, low = parts
    return mm(
        jnp.concatenate([high, low, high], axis=1),
        jnp.concatenate([rhs[0], rhs[0], rhs[1]], axis=0),
    )


def mm3_turned(parts, rhs):
    high, low = parts
    return lax.dot_general(
        jnp.concatenate([high, low, high], axis=1),
        jnp.concatenate([rhs[0], rhs[0], rhs[1]], axis=1),
        (((1,), (1,)), ((), ())),
        preferred_element_type=F32,
    )


def swap_groups(x):
    rows = x.shape[0]
    differ = lax.broadcasted_iota(jnp.int32, x.shape, 0) ^ (
        lax.broadcasted_iota(jnp.int32, x.shape, 1) // GROUP
    )
    group = lax.broadcasted_iota(jnp.int32, x.shape, 1) // GROUP
    for bit in (1, 2, 4):
        up = pltpu.roll(pltpu.roll(x, rows - bit, 0), GROUP * bit, 1)
        down = pltpu.roll(pltpu.roll(x, bit, 0), LANES - GROUP * bit, 1)
        moved = jnp.where((group & bit) != 0, up, down)
        x = jnp.where((differ & bit) == 0, x, moved)
    return x


def to_tiles(arrays):
    return jnp.concatenate(
        [a[:, i : i + LANES] for a in arrays for i in range(0, a.shape[1], LANES)], axis=0
    )


def used_slots(count_ref):
    peers = count_ref.shape[1]
    counts = jnp.broadcast_to(count_ref[...].astype(F32), (peers, peers)).T
    slot = lax.broadcasted_iota(jnp.int32, (peers, LANES), 1) % GROUP
    return slot.astype(F32) < counts


def request_kernel(cell, count, obs, weight, pred, coef_t, bias, send, base):
    peers = count.shape[1]
    coef = jnp.concatenate([coef_t[...], jnp.broadcast_to(bias[...], coef_t.shape)], axis=0).T
    preds = pred.shape[0]
    linear = jnp.broadcast_to(coef[:, preds : preds + 1], obs.shape)
    for i in range(preds):
        linear = linear + coef[:, i : i + 1] * pred[i : i + 1, :]
    base[...] = linear
    target = obs[...] - linear
    cells = jnp.broadcast_to(cell[...].astype(F32), (8, cell.shape[1]))
    packed = swap_groups(
        to_tiles([target[:8], target[8:], weight[:8, :], weight[8:, :], pred[...], cells])
    )
    used = used_slots(count)
    for a in range(6):
        rows = packed[a * peers : (a + 1) * peers]
        if a in (2, 3):
            rows = jnp.where(used, rows, 0.0)
        send[pl.ds(a, peers, stride=ASK), :] = rows


def prepare_kernel(
    state, w_in_t, w_mid_hbm, w_out, s_out, wi, wm, wo_f, wo_b,
    columns, turned, w_mid, wi_v, wm_v, sems, in_sems, out_sems,
):
    feat, rows, cols = state.shape
    hid = w_mid.shape[0]
    chan = w_out.shape[0]
    loads = [
        pltpu.make_async_copy(state.at[:, r, :], columns.at[r, :feat, :], in_sems.at[r])
        for r in range(rows)
    ]
    load_mid = pltpu.make_async_copy(w_mid_hbm, w_mid, sems.at[0])
    for copy in loads[: rows // 2]:
        copy.start()
    load_mid.start()
    for copy in loads[rows // 2 :]:
        copy.start()
    for r in range(rows):
        columns[r, feat:, :] = jnp.zeros((columns.shape[1] - feat, cols), F32)
    w_in = jnp.concatenate([w_in_t[...], jnp.zeros((256 - feat, hid), F32)], axis=0)
    wi_v[0], wi_v[1] = split(w_in)
    stores = [pltpu.make_async_copy(wi_v, wi, sems.at[1])]
    stores[0].start()
    out_high, out_low = split(w_out[...])
    out_high = out_high.astype(F32)
    out_low = out_low.astype(F32)
    stack = jnp.concatenate([out_high, out_low, jnp.zeros((128 - 2 * chan, hid), F32)], axis=0)
    wo_f[...] = stack.T.astype(BF16)
    wo_b[...] = jnp.concatenate(
        [out_high, out_low, out_high, jnp.zeros((128 - 3 * chan, hid), F32)], axis=0
    ).astype(BF16)
    for r in range(rows):
        loads[r].wait()
        block = columns[r].T
        for half in range(2):
            turned[half, r * cols : (r + 1) * cols, :] = block[:, half * 128 : half * 128 + 128]
            store = pltpu.make_async_copy(
                turned.at[half, pl.ds(r * cols, cols), :],
                s_out.at[pl.ds(r * cols, cols), half, :],
                out_sems.at[r, half],
            )
            store.start()
            stores.append(store)
    load_mid.wait()
    wm_v[0], wm_v[1] = split(w_mid[...])
    stores.append(pltpu.make_async_copy(wm_v, wm, sems.at[2]))
    stores[-1].start()
    for store in stores:
        store.wait()


def forward_kernel(
    recv, s0_hbm, wi_hbm, wm_hbm, wo_hbm, b_in, b_mid,
    h1_out, h2_out, r_out, cell_out, send,
    s0, wi, wm, wo, g0, q, w, p, z, moments, cell_smem, sems,
):
    step = pl.program_id(0)
    peers = recv.shape[0] // ASK
    blocks = peers // 8

    def fetch(row, to_row):
        g0[to_row] = s0[row]

    @pl.when(step == 0)
    def _():
        copies = [
            pltpu.make_async_copy(source, target, sems.at[i])
            for i, (source, target) in enumerate(
                ((s0_hbm, s0), (wi_hbm, wi), (wm_hbm, wm), (wo_hbm, wo))
            )
        ]
        for copy in copies:
            copy.start()
        packed = jnp.concatenate([recv[pl.ds(a, peers, stride=ASK), :] for a in range(ASK)], axis=0)
        tiles = swap_groups(packed)

        def tile(a, i):
            return tiles[(a * blocks + i) * 8 : (a * blocks + i) * 8 + 8]

        for i in range(blocks):
            cell_out[i : i + 1, :] = tile(5, i)[0:1].astype(jnp.int32)
        copy = pltpu.make_async_copy(cell_out, cell_smem, sems.at[5])
        copy.start()
        for i in range(blocks):
            lanes = slice(i * LANES, (i + 1) * LANES)
            q[0:8, lanes] = tile(0, i)
            q[8:16, lanes] = tile(1, i)
            w[0:8, lanes] = tile(2, i)
            w[8:16, lanes] = tile(3, i)
            p[:, lanes] = tile(4, i)
        moments[...] = jnp.zeros_like(moments)
        copy.wait()
        copies[0].wait()

        def gather(i, carry):
            for k in range(GROUP):
                fetch(cell_smem[i // 8, (i % 8) * GROUP + k], i * GROUP + k)
            return carry

        for n in range(TILE):
            fetch(cell_smem[n // LANES, n % LANES], n)
        for copy in copies[1:]:
            copy.wait()

    start = pl.multiple_of(step * TILE, TILE)
    here = pl.ds(start, TILE)
    high, low = split(jnp.concatenate([g0[here, 0, :], g0[here, 1, :]], axis=1))
    parts = [slice(j * TILE // 2, (j + 1) * TILE // 2) for j in range(2)]
    h1s = []
    for s in parts:
        h1 = jnp.tanh(mm3((high[s], low[s]), wi) + b_in[...][None, :])
        h1_out[s, :] = h1
        h1s.append(split(h1))
    following = jnp.minimum(step + 1, pl.num_programs(0) - 1)
    for n in range(TILE):
        fetch(
            cell_smem[following * (TILE // LANES) + n // LANES, n % LANES], following * TILE + n
        )
    h2s = []
    for s, hl in zip(parts, h1s):
        h2 = jnp.tanh(mm3_turned(hl, wm) + b_mid[...][None, :])
        h2_out[s, :] = h2
        h2s.append(split(h2))
    total = jnp.concatenate([mm(jnp.concatenate(hl,axis=1), jnp.concatenate([wo[...],wo[...]],axis=0)) for hl in h2s], axis=0).T
    zt = total[0:16] + total[16:32]
    z[:, here] = zt
    residual = w[:, here] * (zt - q[:, here])
    moments[...] += lax.dot_general(
        p[:, here], jnp.concatenate([residual] * 8, axis=0),
        (((1,), (1,)), ((), ())), precision=lax.Precision.HIGHEST, preferred_element_type=F32,
    )
    r_high, r_low = split(residual)
    r_high = r_high.astype(F32)
    r_stack = jnp.concatenate(
        [r_high, r_high, r_low.astype(F32), jnp.zeros((LANES - 48, TILE), F32)], axis=0
    )
    r_out[...] = r_stack.T.astype(BF16)

    @pl.when(step == pl.num_programs(0) - 1)
    def _():
        packed = swap_groups(to_tiles([z[0:8, :], z[8:16, :]]))
        send[pl.ds(0, peers, stride=REPLY), :] = packed[:peers]
        send[pl.ds(1, peers, stride=REPLY), :] = packed[peers:]
        lane_group = lax.broadcasted_iota(jnp.int32, (8, LANES), 1) // GROUP
        own = lane_group == lax.broadcasted_iota(jnp.int32, (8, LANES), 0)
        row = jnp.sum(jnp.where(own, moments[...], 0.0), axis=0, keepdims=True)
        send[pl.ds(2, peers, stride=REPLY), :] = jnp.broadcast_to(row, (peers, LANES))


def backward_kernel(
    cells, h1_hbm, h2_hbm, r, wo_hbm, wm_hbm, wi_hbm, grad,
    h1, h2, wo, wm, wi, i0, i1, a0, a1, c0, c1, out, sems, h1_sems, h2_sems, out_sems,
):
    step = pl.program_id(0)
    last = pl.num_programs(0) - 1
    steps = h1.shape[0] // TILE

    def tile_copy(source, target, some_sems, i):
        rows = pl.ds(pl.multiple_of(i * TILE, TILE), TILE)
        return pltpu.make_async_copy(source.at[rows, :], target.at[rows, :], some_sems.at[i])

    @pl.when(step == 0)
    def _():
        weights = [
            pltpu.make_async_copy(source, target, sems.at[i])
            for i, (source, target) in enumerate(((wo_hbm, wo), (wm_hbm, wm), (wi_hbm, wi)))
        ]
        weights[0].start()
        tile_copy(h2_hbm, h2, h2_sems, 0).start()
        weights[1].start()
        tile_copy(h1_hbm, h1, h1_sems, 0).start()
        weights[2].start()
        for i in range(1, steps):
            tile_copy(h2_hbm, h2, h2_sems, i).start()
            tile_copy(h1_hbm, h1, h1_sems, i).start()
        for acc in (a0, a1, c0, c1, i0, i1):
            acc[...] = jnp.zeros_like(acc)
        for copy in weights:
            copy.wait()

    tile_copy(h2_hbm, h2, h2_sems, step).wait()
    tile_copy(h1_hbm, h1, h1_sems, step).wait()
    start = pl.multiple_of(step * TILE, TILE)

    def add(first, second, n):
        a0[pl.ds(first, 1), :] += i0[pl.ds(n, 1), :]
        a1[pl.ds(first, 1), :] += i1[pl.ds(n, 1), :]
        c0[pl.ds(second, 1), :] += i0[pl.ds(n + 1, 1), :]
        c1[pl.ds(second, 1), :] += i1[pl.ds(n + 1, 1), :]

    before = jnp.maximum(step - 1, 0) * (TILE // LANES)
    for n in range(0, TILE, 2):
        row = before + n // LANES
        add(cells[row, n % LANES], cells[row, n % LANES + 1], n)
    halves = [slice(0, TILE // 2), slice(TILE // 2, TILE)]
    mids = []
    for s in halves:
        x2 = h2[pl.ds(start + s.start, TILE // 2), :]
        mids.append(mm(r[s, :], wo[...]) * (1.0 - x2 * x2))
    ins = []
    for s, back_mid in zip(halves, mids):
        x1 = h1[pl.ds(start + s.start, TILE // 2), :]
        ins.append(mm3(split(back_mid), wm) * (1.0 - x1 * x1))
    for s, back_in in zip(halves, ins):
        increment = mm3_turned(split(back_in), wi)
        i0[s, :] = increment[:, :128]
        i1[s, :] = increment[:, 128:]

    @pl.when(step == last)
    def _():
        def scatter(i, carry):
            row = last * (TILE // LANES) + i // 8
            for k in range(0, GROUP, 2):
                at = (i % 8) * GROUP + k
                add(cells[row, at], cells[row, at + 1], i * GROUP + k)
            return carry

        for n in range(0, TILE, 2):
            row = last * (TILE // LANES) + n // LANES
            add(cells[row, n % LANES], cells[row, n % LANES + 1], n)
        feat, rows, cols = grad.shape
        copies = []
        for row in range(rows):
            at = slice(row * cols, (row + 1) * cols)
            block = jnp.concatenate([a0[at, :] + c0[at, :], a1[at, :] + c1[at, :]], axis=1)
            out[row] = block.T[:feat]
            copies.append(pltpu.make_async_copy(out.at[row], grad.at[:, row, :], out_sems.at[row]))
            copies[-1].start()
        for copy in copies:
            copy.wait()


def finish_kernel(recv, base, count, evolved, bias_grad):
    peers = count.shape[1]
    used = jnp.where(used_slots(count), 1.0, 0.0)
    tiles = swap_groups(
        jnp.concatenate(
            [recv[pl.ds(0, peers, stride=REPLY), :], recv[pl.ds(1, peers, stride=REPLY), :], used], axis=0
        )
    )
    blocks = peers // 8
    for i in range(blocks):
        lanes = slice(i * LANES, (i + 1) * LANES)
        keep = tiles[(2 * blocks + i) * 8 : (2 * blocks + i) * 8 + 8] > 0.5
        for a in range(2):
            value = tiles[(a * blocks + i) * 8 : (a * blocks + i) * 8 + 8]
            rows = slice(8 * a, 8 * a + 8)
            evolved[rows, lanes] = jnp.where(keep, value + base[rows, lanes], 0.0)
    row = jnp.sum(recv[pl.ds(2, peers, stride=REPLY), :], axis=0, keepdims=True)
    lane = lax.broadcasted_iota(jnp.int32, (8, LANES), 1)
    spread = jnp.where(
        lane // GROUP == lax.broadcasted_iota(jnp.int32, (8, LANES), 0),
        jnp.broadcast_to(row, (8, LANES)), 0.0,
    )
    pick = lax.broadcasted_iota(jnp.int32, (LANES, 16), 0) % GROUP == lax.broadcasted_iota(
        jnp.int32, (LANES, 16), 1
    )
    bias_grad[...] = jnp.dot(
        spread, jnp.where(pick, 1.0, 0.0), precision=lax.Precision.HIGHEST,
        preferred_element_type=F32,
    )


def limit(mebibytes):
    return pltpu.CompilerParams(vmem_limit_bytes=mebibytes * 2**20)


def stay(x):
    return pltpu.with_memory_space_constraint(x, pltpu.HBM)


def shape(dims, dtype=F32):
    return pltpu.HBM(dims, dtype)


def exchange(data, peers):
    parts = data.reshape(peers, 1, -1)
    parts = lax.all_to_all(parts, ("gx", "gy"), split_axis=0, concat_axis=0, tiled=True)
    return parts.reshape(data.shape)


def per_device(
    model_state, obs_cell, obs_count, obs_value, obs_weight, predictor, bias_coef,
    weight_in, bias_in, weight_mid, bias_mid, weight_out, bias_out,
):
    feat, rows, cols = model_state.shape
    slots = obs_cell.shape[1]
    peers = obs_count.shape[1]
    hid = weight_mid.shape[0]
    cells = rows * cols
    send, base = pl.pallas_call(
        request_kernel,
        out_shape=(shape((peers * ASK, LANES)), shape((16, slots))),
        name="request",
    )(obs_cell, obs_count, obs_value, obs_weight, predictor, bias_coef.T, bias_out[None, :])
    recv = exchange(send, peers)
    in_hbm = pl.BlockSpec(memory_space=pltpu.HBM)
    in_vmem = pl.BlockSpec(memory_space=pltpu.VMEM)
    s0, wi, wm, wo_f, wo_b = pl.pallas_call(
        prepare_kernel,
        in_specs=[in_hbm, in_vmem, in_hbm, in_vmem],
        out_specs=[in_hbm, in_hbm, in_hbm, in_vmem, in_vmem],
        out_shape=(
            shape((cells, 2, 128)),
            shape((2, 256, hid), BF16), shape((2, hid, hid), BF16),
            shape((hid, 128), BF16), shape((128, hid), BF16),
        ),
        scratch_shapes=[
            pltpu.VMEM((rows, 256, cols), F32), pltpu.VMEM((2, cells, 128), F32),
            pltpu.VMEM((hid, hid), F32),
            pltpu.VMEM((2, 256, hid), BF16), pltpu.VMEM((2, hid, hid), BF16),
            pltpu.SemaphoreType.DMA((3,)), pltpu.SemaphoreType.DMA((rows,)),
            pltpu.SemaphoreType.DMA((rows, 2)),
        ],
        name="prepare",
        cost_estimate=pl.CostEstimate(flops=10**7, transcendentals=0, bytes_accessed=15 * 10**6),
    )(model_state, weight_in.T, weight_mid, weight_out)

    def whole(dims):
        return pl.BlockSpec(dims, lambda i: (0,) * len(dims))

    steps = slots // TILE
    h1, h2, residual, cell, reply = pl.pallas_call(
        forward_kernel,
        grid=(steps,),
        in_specs=[
            whole((peers * ASK, LANES)), in_hbm, in_hbm, in_hbm, in_hbm,
            whole((hid,)), whole((hid,)),
        ],
        out_specs=[
            pl.BlockSpec((TILE, hid), lambda i: (i, 0)),
            pl.BlockSpec((TILE, hid), lambda i: (i, 0)),
            pl.BlockSpec((TILE, 128), lambda i: (i, 0)),
            whole((slots // LANES, LANES)),
            whole((peers * REPLY, LANES)),
        ],
        out_shape=(
            shape((slots, hid)), shape((slots, hid)), shape((slots, 128), BF16),
            shape((slots // LANES, LANES), jnp.int32), shape((peers * REPLY, LANES)),
        ),
        scratch_shapes=[
            pltpu.VMEM((cells, 2, 128), F32),
            pltpu.VMEM((2, 256, hid), BF16), pltpu.VMEM((2, hid, hid), BF16),
            pltpu.VMEM((hid, 128), BF16),
            pltpu.VMEM((slots, 2, 128), F32),
            pltpu.VMEM((16, slots), F32), pltpu.VMEM((16, slots), F32),
            pltpu.VMEM((8, slots), F32), pltpu.VMEM((16, slots), F32),
            pltpu.VMEM((8, LANES), F32),
            pltpu.SMEM((slots // LANES, LANES), jnp.int32),
            pltpu.SemaphoreType.DMA((6,)),
        ],
        name="forward",
        compiler_params=limit(48),
        cost_estimate=pl.CostEstimate(
            flops=6 * slots * hid * (256 + hid + 128), transcendentals=2 * slots * hid,
            bytes_accessed=25 * 10**6,
        ),
    )(recv, *map(stay, (s0, wi, wm, wo_f)), bias_in, bias_mid)
    back = exchange(reply, peers)
    gradient = pl.pallas_call(
        backward_kernel,
        grid=(steps,),
        in_specs=[
            pl.BlockSpec(memory_space=pltpu.SMEM),
            in_hbm, in_hbm,
            pl.BlockSpec((TILE, 128), lambda i: (i, 0)),
            in_hbm, in_hbm, in_hbm,
        ],
        out_specs=in_hbm,
        out_shape=shape((feat, rows, cols)),
        scratch_shapes=[
            pltpu.VMEM((slots, hid), F32), pltpu.VMEM((slots, hid), F32),
            pltpu.VMEM((128, hid), BF16), pltpu.VMEM((2, hid, hid), BF16),
            pltpu.VMEM((2, 256, hid), BF16),
            pltpu.VMEM((TILE, 128), F32), pltpu.VMEM((TILE, 128), F32),
        ]
        + [pltpu.VMEM((cells, 128), F32) for _ in range(4)]
        + [
            pltpu.VMEM((rows, feat, cols), F32),
            pltpu.SemaphoreType.DMA((3,)), pltpu.SemaphoreType.DMA((steps,)),
            pltpu.SemaphoreType.DMA((steps,)), pltpu.SemaphoreType.DMA((rows,)),
        ],
        name="backward",
        cost_estimate=pl.CostEstimate(
            flops=6 * slots * hid * (256 + hid + 128), transcendentals=0,
            bytes_accessed=25 * 10**6,
        ),
    )(cell, h1, h2, residual, wo_b, wm, wi)
    evolved, bias_gradient = pl.pallas_call(
        finish_kernel,
        out_shape=(shape((16, slots)), shape((8, 16))),
        name="finish",
        compiler_params=limit(8),
    )(back, base, obs_count)
    return gradient, evolved, bias_gradient.T


def solution(mesh):
    in_specs = (
        P(None, "gx", "gy"),
        P(("gx", "gy"), None),
        P(("gx", "gy"), None),
        P(None, ("gx", "gy")),
        P(None, ("gx", "gy")),
        P(None, ("gx", "gy")),
        P(),
        P(),
        P(),
        P(),
        P(),
        P(),
        P(),
    )
    out_specs = (P(None, "gx", "gy"), P(None, ("gx", "gy")), P())
    return jax.shard_map(
        per_device, mesh=mesh, in_specs=in_specs, out_specs=out_specs, check_vma=False
    )
```
